32 devices in a mesh: dp: 4 (over z), pipe: 2 (over y), mp: 4 (over x, core).
Axes of the slice: x: 2, y: 2, z: 4, core: 2. Of those that a mesh axis runs over, the one named last changes fastest.
Arguments:
- fwd_in: bfloat16 [2, 512, 1024], P('pipe', ('dp', 'mp')), may hold values from -6 to 6
- grad_in: bfloat16 [2, 512, 1024], P('pipe', ('dp', 'mp')), may hold values from -6 to 6
- saved_in: bfloat16 [2, 512, 1024], P('pipe', ('dp', 'mp')), may hold values from -6 to 6
- saved_hidden: bfloat16 [2, 512, 65536], P('pipe', 'dp', 'mp'), may hold values from -6 to 6
- gain: float32 [2, 1024], P('pipe'), may hold values from 0.25 to 1.75
- w_in: bfloat16 [2, 1024, 65536], P('pipe', None, 'mp'), may hold values from -0.1875 to 0.1875
- w_out: bfloat16 [2, 65536, 1024], P('pipe', 'mp'), may hold values from -0.0234375 to 0.0234375
Outputs:
- fwd_out: bfloat16 [2, 512, 1024], P('pipe', ('dp', 'mp'))
- grad_out: bfloat16 [2, 512, 1024], P('pipe', ('dp', 'mp'))
The draws below stay inside these ranges and needn't reach their ends.
All inputs are finite; a program needn't handle non-finite values.
Results may differ from the reference program's by a relative error of at most 0.008.
Values may be sent and summed in bfloat16 or wider, within the bound.
No kernel may reach another device: no remote copies, remote signals or barrier semaphores. Data moves between devices by JAX's collectives and lax.ppermute only.
A program may use at most 192 MiB of HBM per device.

```python
import jax
import jax.numpy as jnp
from jax import lax

D = 1024
FF = 65536
TOKENS = 512
SECTIONS = 2
N_MP = 4


def steps_of(own_key, dims, shards, low, largest):
    level = 1.0
    for axis_at, shards_of in shards:
        steps = jax.random.uniform(jax.random.fold_in(jax.random.fold_in(own_key, 6), axis_at), (shards_of,), jnp.float32, low / len(shards), largest / len(shards))
        level = level * jnp.repeat(jnp.exp(steps), dims[axis_at] // shards_of).reshape((-1,) + (1,) * (len(dims) - 1 - axis_at))
    return level


def normal_values(rng, extent, deviation, reach, shards=(), kind=jnp.bfloat16):
    level = steps_of(rng, extent, shards, -0.22, 0.18) if shards else 1.0
    values = jax.random.normal(rng, extent, jnp.float32) * deviation * level
    return jnp.minimum(jnp.maximum(values, -reach), reach).astype(kind)


def setup_inputs(seed: int = 0) -> dict:
    streams_of = jax.random.split(jax.random.key(seed), 8)
    fwd_in = normal_values(streams_of[0], (SECTIONS, TOKENS, D), 1.0, 6.0, ((0, 2), (1, 16)))
    grad_in = normal_values(streams_of[1], (SECTIONS, TOKENS, D), 1.0, 6.0, ((0, 2), (1, 16)))
    saved_in = normal_values(streams_of[2], (SECTIONS, TOKENS, D), 1.0, 6.0, ((0, 2), (1, 16)))
    saved_hidden = normal_values(streams_of[3], (SECTIONS, TOKENS, FF), 1.0, 6.0, ((0, 2), (1, 4), (2, 4)))
    gain = jnp.clip(1.0 + 0.15 * jax.random.normal(streams_of[4], (SECTIONS, D), jnp.float32), 0.25, 1.75)
    w_in = normal_values(streams_of[5], (SECTIONS, D, FF), D ** -0.5, 0.1875, ((0, 2), (2, 4)))
    w_out = normal_values(streams_of[6], (SECTIONS, FF, D), FF ** -0.5, 0.0234375, ((0, 2), (1, 4)))
    return {"fwd_in": fwd_in, "grad_in": grad_in, "saved_in": saved_in, "saved_hidden": saved_hidden, "gain": gain, "w_in": w_in, "w_out": w_out}


def rounded(value):
    low = lax.optimization_barrier(value.astype(jnp.bfloat16))
    return low.astype(jnp.float32)

def one_section(args):
    x, g, u, saved, scale, win, wout = args
    xf = x.astype(jnp.float32)
    normed = (xf * lax.rsqrt(lax.optimization_barrier(jnp.mean(xf * xf, axis=-1, keepdims=True)) + 1e-06) * scale).astype(jnp.bfloat16)
    hidden = jnp.maximum(jnp.dot(normed, win, preferred_element_type=jnp.float32), 0.0).astype(jnp.bfloat16)
    back = lax.dot_general(g, wout, (((1,), (1,)), ((), ())), preferred_element_type=jnp.float32)
    hidden_grad = jnp.where(saved > 0, back, 0.0).astype(jnp.bfloat16)
    block = FF // N_MP

    def add_block(carry, index):
        fwd_total, bwd_total = carry
        start = (index * block).astype(jnp.int32)
        hid_block = lax.dynamic_slice_in_dim(hidden, start, block, 1)
        out_rows = lax.dynamic_slice_in_dim(wout, start, block, 0)
        grad_block = lax.dynamic_slice_in_dim(hidden_grad, start, block, 1)
        in_cols = lax.dynamic_slice_in_dim(win, start, block, 1)
        fwd_part = jnp.dot(hid_block, out_rows, preferred_element_type=jnp.float32)
        bwd_part = lax.dot_general(grad_block, in_cols, (((1,), (1,)), ((), ())), preferred_element_type=jnp.float32)
        return ((fwd_total + rounded(fwd_part), bwd_total + rounded(bwd_part)), None)
    zeros = jnp.zeros((x.shape[0], x.shape[1]), jnp.float32)
    (projected, normed_grad), _ = lax.scan(add_block, (zeros, zeros), jnp.arange(N_MP, dtype=jnp.int32))
    section_out = (xf + projected).astype(jnp.bfloat16)
    uf = u.astype(jnp.float32)
    recip = lax.rsqrt(lax.optimization_barrier(jnp.mean(uf * uf, axis=-1, keepdims=True)) + 1e-06)
    scaled = normed_grad * scale
    inner = lax.optimization_barrier(jnp.mean(scaled * uf, axis=-1, keepdims=True))
    input_grad = (g.astype(jnp.float32) + recip * scaled - uf * recip * recip * recip * inner).astype(jnp.bfloat16)
    return (section_out, input_grad)

def reference(fwd_in, grad_in, saved_in, saved_hidden, gain, w_in, w_out):
    outs, grads = lax.map(one_section, (fwd_in, grad_in, saved_in, saved_hidden, gain[:, None, :], w_in, w_out))
    return (jnp.roll(outs, 1, axis=0), jnp.roll(grads, -1, axis=0))
```

```python
import functools

import jax
import jax.numpy as jnp
from jax import lax
from jax.experimental import pallas as pl
from jax.experimental.pallas import tpu as pltpu
from jax.sharding import PartitionSpec as P

EPS = 1e-06
NT = (((1,), (1,)), ((), ()))
F32 = jnp.float32
BF16 = jnp.bfloat16


def tile_of(extent, limit):
    size = limit
    while size > 128 and extent % size:
        size //= 2
    return size if extent % size == 0 else extent


def section_kernel(tiles, x_ref, g_ref, scale_ref, s_ref, wi_ref, wo_ref, of_ref, ob_ref, n_ref, af, ab):
    step = pl.program_id(0)

    @pl.when(step == 0)
    def _():
        xf = x_ref[...].astype(F32)
        r = lax.rsqrt(jnp.mean(xf * xf, axis=-1, keepdims=True) + EPS)
        n_ref[...] = (xf * r * scale_ref[...]).astype(BF16)
        af[...] = jnp.zeros_like(af)
        ab[...] = jnp.zeros_like(ab)

    h = jnp.maximum(jnp.dot(n_ref[...], wi_ref[...], preferred_element_type=F32), 0.0).astype(BF16)
    af[...] += jnp.dot(h, wo_ref[...], preferred_element_type=F32)
    p = lax.dot_general(g_ref[...], wo_ref[...], NT, preferred_element_type=F32)
    hg = jnp.where(s_ref[...] > 0, p, 0.0).astype(BF16)
    ab[...] += lax.dot_general(hg, wi_ref[...], NT, preferred_element_type=F32)

    @pl.when(step == tiles - 1)
    def _():
        of_ref[...] = af[...].astype(BF16)
        ob_ref[...] = ab[...].astype(BF16)


def section(x, g, scale, saved, w_in, w_out):
    tokens, width = x.shape
    hidden = w_in.shape[1]
    tile = tile_of(hidden, 1024)
    tiles = hidden // tile
    whole = pl.BlockSpec((tokens, width), lambda i: (0, 0))
    out = jax.ShapeDtypeStruct((tokens, width), BF16)
    return pl.pallas_call(
        functools.partial(section_kernel, tiles),
        grid=(tiles,),
        in_specs=[
            whole,
            whole,
            pl.BlockSpec((1, width), lambda i: (0, 0)),
            pl.BlockSpec((tokens, tile), lambda i: (0, i)),
            pl.BlockSpec((width, tile), lambda i: (0, i)),
            pl.BlockSpec((tile, width), lambda i: (i, 0)),
        ],
        out_specs=[whole, whole],
        out_shape=[out, out],
        scratch_shapes=[
            pltpu.VMEM((tokens, width), BF16),
            pltpu.VMEM((tokens, width), F32),
            pltpu.VMEM((tokens, width), F32),
        ],
        compiler_params=pltpu.CompilerParams(
            dimension_semantics=("arbitrary",), vmem_limit_bytes=48 << 20
        ),
        cost_estimate=pl.CostEstimate(
            flops=8 * tokens * width * hidden,
            bytes_accessed=4 * width * hidden + 2 * tokens * hidden,
            transcendentals=0,
        ),
        name="section",
    )(x, g, scale, saved, w_in, w_out)


def shifted(block, axis, distance):
    devices = range(lax.axis_size(axis))
    route = [((i - distance) % len(devices), i) for i in devices]
    return lax.ppermute(block, axis, route)


def gathered(block, axis):
    size = lax.axis_size(axis)
    rows = block.shape[0]
    me = lax.axis_index(axis)
    full = jnp.zeros((size * rows,) + block.shape[1:], block.dtype)
    full = lax.dynamic_update_slice(full, block, (me * rows, 0))
    for distance in range(1, size):
        got = shifted(block, axis, distance)
        full = lax.dynamic_update_slice(full, got, (((me - distance) % size) * rows, 0))
    return full


def scattered(full, axis):
    size = lax.axis_size(axis)
    rows = full.shape[0] // size
    me = lax.axis_index(axis)
    total = lax.dynamic_slice(full, (me * rows, 0), (rows, full.shape[1])).astype(F32)
    for distance in range(1, size):
        part = lax.dynamic_slice(full, (((me + distance) % size) * rows, 0), (rows, full.shape[1]))
        total = total + shifted(part, axis, distance).astype(F32)
    return total


def on_device(fwd_in, grad_in, saved_in, saved_hidden, gain, w_in, w_out):
    scale = gain[0][None, :]
    x, g, u = fwd_in[0], grad_in[0], saved_in[0]
    out_part, grad_part = section(
        gathered(x, "mp"), gathered(g, "mp"), scale, saved_hidden[0], w_in[0], w_out[0]
    )
    projected = scattered(out_part, "mp")
    normed_grad = scattered(grad_part, "mp")
    section_out = (x.astype(F32) + projected).astype(BF16)
    uf = u.astype(F32)
    recip = lax.rsqrt(jnp.mean(uf * uf, axis=-1, keepdims=True) + EPS)
    scaled = normed_grad * scale
    inner = jnp.mean(scaled * uf, axis=-1, keepdims=True)
    input_grad = (g.astype(F32) + recip * scaled - uf * recip * recip * recip * inner).astype(BF16)
    return (shifted(section_out, "pipe", 1)[None], shifted(input_grad, "pipe", -1)[None])


def solution(mesh):
    rows = P("pipe", ("dp", "mp"), None)
    in_specs = (
        rows,
        rows,
        rows,
        P("pipe", "dp", "mp"),
        P("pipe", None),
        P("pipe", None, "mp"),
        P("pipe", "mp", None),
    )
    return jax.shard_map(
        on_device, mesh=mesh, in_specs=in_specs, out_specs=(rows, rows), check_vma=False
    )
```

```python
import functools

import jax
import jax.numpy as jnp
from jax import lax
from jax.experimental import pallas as pl
from jax.experimental.pallas import tpu as pltpu
from jax.sharding import PartitionSpec as P

EPS = 1e-06
F32 = jnp.float32
BF16 = jnp.bfloat16


def tile_of(extent, limit):
    size = limit
    while size > 128 and extent % size:
        size //= 2
    return size if extent % size == 0 else extent


def section_kernel(tiles, rows, parts, outs, me_ref, *refs):
    blocks, refs = refs[:parts], refs[parts:]
    scale_ref, s_ref, wi_ref, wo_ref = refs[:4]
    out_refs, refs = refs[4 : 4 + outs], refs[4 + outs :]
    n_ref, g_ref, af, ab, wit, wot = refs
    step = pl.program_id(0)
    me = me_ref[0]

    def place(k):
        return pl.ds(pl.multiple_of((me ^ k) * rows, rows), rows)

    @pl.when(step == 0)
    def _():
        for k, block in enumerate(blocks):
            xf = block[0].astype(F32)
            r = lax.rsqrt(jnp.mean(xf * xf, axis=-1, keepdims=True) + EPS)
            n_ref[place(k), :] = (xf * r * scale_ref[...]).astype(BF16)
            g_ref[place(k), :] = block[1]
        af[...] = jnp.zeros_like(af)
        ab[...] = jnp.zeros_like(ab)

    wot[...] = wo_ref[...].T
    h = jnp.maximum(jnp.dot(n_ref[...], wi_ref[...], preferred_element_type=F32), 0.0).astype(BF16)
    af[...] += jnp.dot(h, wo_ref[...], preferred_element_type=F32)
    p = jnp.dot(g_ref[...], wot[...], preferred_element_type=F32)
    hg = jnp.where(s_ref[...] > 0, p, 0.0).astype(BF16)
    wit[...] = wi_ref[...].T
    ab[...] += jnp.dot(hg, wit[...], preferred_element_type=F32)

    @pl.when(step == tiles - 1)
    def _():
        for k in range(parts):
            out = out_refs[k % outs]
            out[k // outs, 0] = af[place(k), :].astype(BF16)
            out[k // outs, 1] = (ab[place(k), :] * scale_ref[...]).astype(BF16)


def section(me, blocks, scale, saved, w_in, w_out):
    parts = len(blocks)
    _, rows, width = blocks[0].shape
    tokens = parts * rows
    hidden = w_in.shape[1]
    tile = tile_of(hidden, 2048)
    tiles = hidden // tile
    outs = min(parts, 2)
    per = parts // outs
    block = pl.BlockSpec((2, rows, width), lambda i, me: (0, 0, 0))
    out = jax.ShapeDtypeStruct((per, 2, rows, width), BF16)
    return pl.pallas_call(
        functools.partial(section_kernel, tiles, rows, parts, outs),
        grid_spec=pltpu.PrefetchScalarGridSpec(
            num_scalar_prefetch=1,
            grid=(tiles,),
            in_specs=[block] * parts
            + [
                pl.BlockSpec((1, width), lambda i, me: (0, 0)),
                pl.BlockSpec((tokens, tile), lambda i, me: (0, i)),
                pl.BlockSpec((width, tile), lambda i, me: (0, i)),
                pl.BlockSpec((tile, width), lambda i, me: (i, 0)),
            ],
            out_specs=[pl.BlockSpec((per, 2, rows, width), lambda i, me: (0, 0, 0, 0))] * outs,
            scratch_shapes=[
                pltpu.VMEM((tokens, width), BF16),
                pltpu.VMEM((tokens, width), BF16),
                pltpu.VMEM((tokens, width), F32),
                pltpu.VMEM((tokens, width), F32),
                pltpu.VMEM((tile, width), BF16),
                pltpu.VMEM((width, tile), BF16),
            ],
        ),
        out_shape=[out] * outs,
        compiler_params=pltpu.CompilerParams(
            dimension_semantics=("arbitrary",), vmem_limit_bytes=52 << 20
        ),
        cost_estimate=pl.CostEstimate(
            flops=8 * tokens * width * hidden,
            bytes_accessed=4 * width * hidden + 2 * tokens * hidden,
            transcendentals=0,
        ),
        name="section",
    )(me, *blocks, scale, saved, w_in, w_out)


def sent(block, pipe_step, mp_xor):
    pipes, size = lax.axis_size("pipe"), lax.axis_size("mp")
    route = [
        (p * size + m, ((p + pipe_step) % pipes) * size + (m ^ mp_xor))
        for p in range(pipes)
        for m in range(size)
    ]
    return lax.ppermute(block, ("pipe", "mp"), route)


def onward(pair):
    return moved(pair, 0)


def moved(pair, mp_xor):
    if lax.axis_size("pipe") <= 2:
        return sent(pair, 1, mp_xor)
    return jnp.concatenate([sent(pair[:1], 1, mp_xor), sent(pair[1:], -1, mp_xor)])


def exchanged(own, size):
    blocks = {0: own}
    bit = size // 2
    while bit:
        for k in list(blocks):
            blocks[k ^ bit] = sent(blocks[k], 0, bit)
        bit //= 2
    return [blocks[k] for k in range(size)]


def rows_onward(x, g, u):
    if lax.axis_size("pipe") <= 2:
        return sent(jnp.stack([x, g, u]), 1, 0)
    return jnp.concatenate([sent(x[None], 1, 0), sent(jnp.stack([g, u]), -1, 0)])


def on_device(fwd_in, grad_in, saved_in, saved_hidden, gain, w_in, w_out):
    scale = gain[0][None, :]
    x, g, u = fwd_in[0], grad_in[0], saved_in[0]
    shifted = rows_onward(x, g, u)
    size = lax.axis_size("mp")
    rows = x.shape[0]
    own = jnp.stack([x, g])
    weights = (scale, saved_hidden[0], w_in[0], w_out[0])
    if size & (size - 1) == 0 and size > 1 and rows % 16 == 0:
        me = jnp.full((1,), lax.axis_index("mp"), jnp.int32)
        keep, give = section(me, exchanged(own, size), *weights)
        got = sent(give, 0, 1)
        total = jnp.zeros((2,) + x.shape, F32)
        for k in range(size // 2):
            pair = (keep[k].astype(F32) + got[k].astype(F32)).astype(BF16)
            total = total + moved(pair, 2 * k).astype(F32)
    else:
        whole = lax.all_gather(own, "mp", axis=1, tiled=True)
        (part,) = section(jnp.zeros((1,), jnp.int32), [whole], *weights)
        total = onward(lax.psum_scatter(part[0], "mp", scatter_dimension=1, tiled=True)).astype(F32)
    x, g, u = shifted
    section_out = (x.astype(F32) + total[0]).astype(BF16)
    uf = u.astype(F32)
    recip = lax.rsqrt(jnp.mean(uf * uf, axis=-1, keepdims=True) + EPS)
    scaled = total[1]
    inner = jnp.mean(scaled * uf, axis=-1, keepdims=True)
    input_grad = (g.astype(F32) + recip * scaled - uf * recip * recip * recip * inner).astype(BF16)
    return (section_out[None], input_grad[None])


def solution(mesh):
    rows = P("pipe", ("dp", "mp"), None)
    in_specs = (
        rows,
        rows,
        rows,
        P("pipe", "dp", "mp"),
        P("pipe", None),
        P("pipe", None, "mp"),
        P("pipe", "mp", None),
    )
    return jax.shard_map(
        on_device, mesh=mesh, in_specs=in_specs, out_specs=(rows, rows), check_vma=False
    )
```

```python
import functools

import jax
import jax.numpy as jnp
from jax import lax
from jax.experimental import pallas as pl
from jax.experimental.pallas import tpu as pltpu
from jax.sharding import PartitionSpec as P

EPS = 1e-06
F32 = jnp.float32
BF16 = jnp.bfloat16


def tile_of(extent, limit):
    size = limit
    while size > 128 and extent % size:
        size //= 2
    return size if extent % size == 0 else extent


def pack_kernel(x_ref, g_ref, u_ref, gain_ref, own_ref, all_ref, scale_ref):
    x, g = x_ref[...], g_ref[...]
    xf = x.astype(F32)
    r = lax.rsqrt(jnp.mean(xf * xf, axis=-1, keepdims=True) + EPS)
    own_ref[0] = (xf * r * gain_ref[...]).astype(BF16)
    own_ref[1] = g
    all_ref[0] = x
    all_ref[1] = g
    all_ref[2] = u_ref[...]
    scale_ref[...] = gain_ref[...]


def packed(x, g, u, gain):
    return pl.pallas_call(
        pack_kernel,
        out_shape=[
            pltpu.VMEM((2,) + x.shape, BF16),
            pltpu.VMEM((3,) + x.shape, BF16),
            pltpu.VMEM(gain.shape, F32),
        ],
        name="pack",
    )(x, g, u, gain)


def tile_copies(tile, at, sources, targets, sems):
    wi, wo = sources
    cut = pl.ds(at * tile if isinstance(at, int) else pl.multiple_of(at * tile, tile), tile)
    return [
        pltpu.make_async_copy(wi.at[:, cut], targets[0], sems.at[0]),
        pltpu.make_async_copy(wo.at[cut, :], targets[1], sems.at[1]),
    ]


def load_kernel(tile, wi_hbm, wo_hbm, wi_ref, wo_ref, sems):
    copies = tile_copies(tile, 0, (wi_hbm, wo_hbm), (wi_ref, wo_ref), sems)
    for copy in copies:
        copy.start()
    for copy in copies:
        copy.wait()


def first_tile(tile, w_in, w_out):
    width = w_in.shape[0]
    return pl.pallas_call(
        functools.partial(load_kernel, tile),
        in_specs=[pl.BlockSpec(memory_space=pltpu.HBM)] * 2,
        out_specs=[pl.BlockSpec(memory_space=pltpu.VMEM)] * 2,
        out_shape=[pltpu.VMEM((width, tile), BF16), pltpu.VMEM((tile, width), BF16)],
        scratch_shapes=[pltpu.SemaphoreType.DMA((2,))],
        compiler_params=pltpu.CompilerParams(vmem_limit_bytes=24 << 20),
        cost_estimate=pl.CostEstimate(
            flops=0, bytes_accessed=8 * tile * width, transcendentals=0
        ),
        name="load",
    )(w_in, w_out)


def section_kernel(tiles, tile, rows, parts, outs, me_ref, *refs):
    blocks, refs = refs[:parts], refs[parts:]
    scale_ref, s_ref, refs = refs[0], refs[1], refs[2:]
    first, sources, refs = refs[:2], refs[2:4], refs[4:]
    out_refs, refs = refs[:outs], refs[outs:]
    n_ref, g_ref, af, ab, wit, wot, wi_buf, wo_buf, sems = refs
    step = pl.program_id(0)
    me = me_ref[0]

    def place(k):
        return pl.ds(pl.multiple_of((me ^ k) * rows, rows), rows)

    def fetch(at, slot):
        targets = (wi_buf.at[slot], wo_buf.at[slot])
        return tile_copies(tile, at, sources, targets, sems.at[slot])

    def compute(wi, wo):
        half = tile // 2
        low, high = slice(0, half), slice(half, tile)

        def hidden(cut):
            h = jnp.dot(n_ref[...], wi[:, cut], preferred_element_type=F32)
            return jnp.maximum(h, 0.0).astype(BF16)

        def hidden_grad(cut):
            p = jnp.dot(g_ref[...], wot[:, cut], preferred_element_type=F32)
            at = pl.multiple_of(step * tile + cut.start, half)
            return jnp.where(s_ref[:, pl.ds(at, half)] > 0, p, 0.0).astype(BF16)

        wot[:, low] = wo[low, :].T
        h = hidden(low)
        wit[low, :] = wi[:, low].T
        af[...] += jnp.dot(h, wo[low, :], preferred_element_type=F32)
        wot[:, high] = wo[high, :].T
        hg = hidden_grad(low)
        h = hidden(high)
        wit[high, :] = wi[:, high].T
        ab[...] += jnp.dot(hg, wit[low, :], preferred_element_type=F32)
        af[...] += jnp.dot(h, wo[high, :], preferred_element_type=F32)
        ab[...] += jnp.dot(hidden_grad(high), wit[high, :], preferred_element_type=F32)

    @pl.when(step == 0)
    def _():
        for at in range(1, min(3, tiles)):
            for copy in fetch(at, at % 2):
                copy.start()
        for k, block in enumerate(blocks):
            n_ref[place(k), :] = block[0]
            g_ref[place(k), :] = block[1]
        af[...] = jnp.zeros_like(af)
        ab[...] = jnp.zeros_like(ab)
        compute(*first)

    @pl.when(step > 0)
    def _():
        slot = lax.rem(step, 2)
        for copy in fetch(step, slot):
            copy.wait()
        compute(wi_buf.at[slot], wo_buf.at[slot])

        @pl.when(step + 2 < tiles)
        def _():
            for copy in fetch(step + 2, slot):
                copy.start()

    @pl.when(step == tiles - 1)
    def _():
        for k in range(parts):
            out = out_refs[k % outs]
            out[k // outs, 0] = af[place(k), :].astype(BF16)
            out[k // outs, 1] = (ab[place(k), :] * scale_ref[...]).astype(BF16)


def section(tile, me, blocks, scale, first, saved, w_in, w_out):
    parts = len(blocks)
    _, rows, width = blocks[0].shape
    tokens = parts * rows
    hidden = w_in.shape[1]
    tiles = hidden // tile
    outs = min(parts, 2)
    per = parts // outs
    inside = pl.BlockSpec(memory_space=pltpu.VMEM)
    outside = pl.BlockSpec(memory_space=pltpu.HBM)
    out = jax.ShapeDtypeStruct((per, 2, rows, width), BF16)
    return pl.pallas_call(
        functools.partial(section_kernel, tiles, tile, rows, parts, outs),
        grid_spec=pltpu.PrefetchScalarGridSpec(
            num_scalar_prefetch=1,
            grid=(tiles,),
            in_specs=[inside] * (parts + 4) + [outside] * 2,
            out_specs=[inside] * outs,
            scratch_shapes=[
                pltpu.VMEM((tokens, width), BF16),
                pltpu.VMEM((tokens, width), BF16),
                pltpu.VMEM((tokens, width), F32),
                pltpu.VMEM((tokens, width), F32),
                pltpu.VMEM((tile, width), BF16),
                pltpu.VMEM((width, tile), BF16),
                pltpu.VMEM((2, width, tile), BF16),
                pltpu.VMEM((2, tile, width), BF16),
                pltpu.SemaphoreType.DMA((2, 2)),
            ],
        ),
        out_shape=[out] * outs,
        compiler_params=pltpu.CompilerParams(
            dimension_semantics=("arbitrary",), vmem_limit_bytes=36 << 20
        ),
        cost_estimate=pl.CostEstimate(
            flops=8 * tokens * width * hidden,
            bytes_accessed=4 * width * hidden + 2 * tokens * hidden,
            transcendentals=0,
        ),
        name="section",
    )(me, *blocks, scale, saved, *first, w_in, w_out)


def sent(block, pipe_step, mp_xor):
    pipes, size = lax.axis_size("pipe"), lax.axis_size("mp")
    route = [
        (p * size + m, ((p + pipe_step) % pipes) * size + (m ^ mp_xor))
        for p in range(pipes)
        for m in range(size)
    ]
    return lax.ppermute(block, ("pipe", "mp"), route)


def onward(pair):
    return moved(pair, 0)


def moved(pair, mp_xor):
    if lax.axis_size("pipe") <= 2:
        return sent(pair, 1, mp_xor)
    return jnp.concatenate([sent(pair[:1], 1, mp_xor), sent(pair[1:], -1, mp_xor)])


def exchanged(own, size):
    blocks = {0: own}
    for k in sorted(range(1, size), key=lambda k: -k):
        blocks[k] = sent(own, 0, k)
    return [blocks[k] for k in range(size)]


def rows_onward(three):
    if lax.axis_size("pipe") <= 2:
        return sent(three, 1, 0)
    return jnp.concatenate([sent(three[:1], 1, 0), sent(three[1:], -1, 0)])


def on_device(fwd_in, grad_in, saved_in, saved_hidden, gain, w_in, w_out):
    own, three, scale = packed(fwd_in[0], grad_in[0], saved_in[0], gain[0][None, :])
    shifted = rows_onward(three)
    size = lax.axis_size("mp")
    rows = own.shape[1]
    arrays = (saved_hidden[0], w_in[0], w_out[0])
    tile = tile_of(w_in.shape[2], 2048)
    first = first_tile(tile, *arrays[1:])
    if size & (size - 1) == 0 and size > 1 and rows % 16 == 0:
        me = jnp.full((1,), lax.axis_index("mp"), jnp.int32)
        keep, give = section(tile, me, exchanged(own, size), scale, first, *arrays)
        got = sent(give, 0, 1)
        total = jnp.zeros((2,) + own.shape[1:], F32)
        for k in range(size // 2):
            pair = (keep[k].astype(F32) + got[k].astype(F32)).astype(BF16)
            total = total + moved(pair, 2 * k).astype(F32)
    else:
        whole = lax.all_gather(own, "mp", axis=1, tiled=True)
        me = jnp.zeros((1,), jnp.int32)
        (part,) = section(tile, me, [whole], scale, first, *arrays)
        total = onward(lax.psum_scatter(part[0], "mp", scatter_dimension=1, tiled=True)).astype(F32)
    x, g, u = shifted
    section_out = (x.astype(F32) + total[0]).astype(BF16)
    uf = u.astype(F32)
    recip = lax.rsqrt(jnp.mean(uf * uf, axis=-1, keepdims=True) + EPS)
    scaled = total[1]
    inner = jnp.mean(scaled * uf, axis=-1, keepdims=True)
    input_grad = (g.astype(F32) + recip * scaled - uf * recip * recip * recip * inner).astype(BF16)
    return (section_out[None], input_grad[None])


def solution(mesh):
    rows = P("pipe", ("dp", "mp"), None)
    in_specs = (
        rows,
        rows,
        rows,
        P("pipe", "dp", "mp"),
        P("pipe", None),
        P("pipe", None, "mp"),
        P("pipe", "mp", None),
    )
    return jax.shard_map(
        on_device, mesh=mesh, in_specs=in_specs, out_specs=(rows, rows), check_vma=False
    )
```

```python
import functools

import jax
import jax.numpy as jnp
from jax import lax
from jax.experimental import pallas as pl
from jax.experimental.pallas import tpu as pltpu
from jax.sharding import PartitionSpec as P

EPS = 1e-06
F32 = jnp.float32
BF16 = jnp.bfloat16


def tile_of(extent, limit):
    size = limit
    while size > 128 and extent % size:
        size //= 2
    return size if extent % size == 0 else extent


def pack_kernel(x_ref, g_ref, u_ref, gain_ref, own_ref, all_ref, scale_ref):
    x, g = x_ref[...], g_ref[...]
    xf = x.astype(F32)
    r = lax.rsqrt(jnp.mean(xf * xf, axis=-1, keepdims=True) + EPS)
    own_ref[0] = (xf * r * gain_ref[...]).astype(BF16)
    own_ref[1] = g
    all_ref[0] = x
    all_ref[1] = g
    all_ref[2] = u_ref[...]
    scale_ref[...] = gain_ref[...]


def packed(x, g, u, gain):
    return pl.pallas_call(
        pack_kernel,
        out_shape=[
            pltpu.VMEM((2,) + x.shape, BF16),
            pltpu.VMEM((3,) + x.shape, BF16),
            pltpu.VMEM(gain.shape, F32),
        ],
        name="pack",
    )(x, g, u, gain)


def tile_copies(tile, at, sources, targets, sems):
    wi, wo = sources
    cut = pl.ds(at * tile if isinstance(at, int) else pl.multiple_of(at * tile, tile), tile)
    return [
        pltpu.make_async_copy(wi.at[:, cut], targets[0], sems.at[0]),
        pltpu.make_async_copy(wo.at[cut, :], targets[1], sems.at[1]),
    ]


def load_kernel(tile, wi_hbm, wo_hbm, wi_ref, wo_ref, sems):
    copies = tile_copies(tile, 0, (wi_hbm, wo_hbm), (wi_ref, wo_ref), sems)
    for copy in copies:
        copy.start()
    for copy in copies:
        copy.wait()


def first_tile(tile, w_in, w_out):
    width = w_in.shape[0]
    return pl.pallas_call(
        functools.partial(load_kernel, tile),
        in_specs=[pl.BlockSpec(memory_space=pltpu.HBM)] * 2,
        out_specs=[pl.BlockSpec(memory_space=pltpu.VMEM)] * 2,
        out_shape=[pltpu.VMEM((width, tile), BF16), pltpu.VMEM((tile, width), BF16)],
        scratch_shapes=[pltpu.SemaphoreType.DMA((2,))],
        compiler_params=pltpu.CompilerParams(vmem_limit_bytes=24 << 20),
        cost_estimate=pl.CostEstimate(
            flops=0, bytes_accessed=8 * tile * width, transcendentals=0
        ),
        name="load",
    )(w_in, w_out)


def section_kernel(tiles, tile, depth, rows, parts, outs, me_ref, *refs):
    blocks, refs = refs[:parts], refs[parts:]
    scale_ref, s_ref, refs = refs[0], refs[1], refs[2:]
    first, sources, refs = refs[:2], refs[2:4], refs[4:]
    out_refs, refs = refs[:outs], refs[outs:]
    n_ref, g_ref, af, ab, wit, wot, wi_buf, wo_buf, sems = refs
    step = pl.program_id(0)
    me = me_ref[0]

    def place(k):
        return pl.ds(pl.multiple_of((me ^ k) * rows, rows), rows)

    def fetch(at, slot):
        targets = (wi_buf.at[slot], wo_buf.at[slot])
        return tile_copies(tile, at, sources, targets, sems.at[slot])

    def compute(wi, wo):
        half = tile // 2
        low, high = slice(0, half), slice(half, tile)

        def hidden(cut):
            h = jnp.dot(n_ref[...], wi[:, cut], preferred_element_type=F32)
            return jnp.maximum(h, 0.0).astype(BF16)

        def hidden_grad(cut):
            p = jnp.dot(g_ref[...], wot[:, cut], preferred_element_type=F32)
            at = pl.multiple_of(step * tile + cut.start, half)
            return jnp.where(s_ref[:, pl.ds(at, half)] > 0, p, 0.0).astype(BF16)

        wot[:, low] = wo[low, :].T
        h = hidden(low)
        wit[low, :] = wi[:, low].T
        af[...] += jnp.dot(h, wo[low, :], preferred_element_type=F32)
        wot[:, high] = wo[high, :].T
        hg = hidden_grad(low)
        h = hidden(high)
        wit[high, :] = wi[:, high].T
        ab[...] += jnp.dot(hg, wit[low, :], preferred_element_type=F32)
        af[...] += jnp.dot(h, wo[high, :], preferred_element_type=F32)
        ab[...] += jnp.dot(hidden_grad(high), wit[high, :], preferred_element_type=F32)

    @pl.when(step == 0)
    def _():
        for at in range(1, min(depth + 1, tiles)):
            for copy in fetch(at, at % depth):
                copy.start()
        for k, block in enumerate(blocks):
            n_ref[place(k), :] = block[0]
            g_ref[place(k), :] = block[1]
        af[...] = jnp.zeros_like(af)
        ab[...] = jnp.zeros_like(ab)
        compute(*first)

    @pl.when(step > 0)
    def _():
        slot = lax.rem(step, depth)
        for copy in fetch(step, slot):
            copy.wait()
        compute(wi_buf.at[slot], wo_buf.at[slot])

        @pl.when(step + depth < tiles)
        def _():
            for copy in fetch(step + depth, slot):
                copy.start()

    @pl.when(step == tiles - 1)
    def _():
        for k in range(parts):
            out = out_refs[k % outs]
            out[k // outs, 0] = af[place(k), :].astype(BF16)
            out[k // outs, 1] = (ab[place(k), :] * scale_ref[...]).astype(BF16)


def section(tile, me, blocks, scale, first, saved, w_in, w_out):
    parts = len(blocks)
    _, rows, width = blocks[0].shape
    tokens = parts * rows
    hidden = w_in.shape[1]
    tiles = hidden // tile
    depth = 2
    outs = min(parts, 2)
    per = parts // outs
    inside = pl.BlockSpec(memory_space=pltpu.VMEM)
    outside = pl.BlockSpec(memory_space=pltpu.HBM)
    out = jax.ShapeDtypeStruct((per, 2, rows, width), BF16)
    return pl.pallas_call(
        functools.partial(section_kernel, tiles, tile, depth, rows, parts, outs),
        grid_spec=pltpu.PrefetchScalarGridSpec(
            num_scalar_prefetch=1,
            grid=(tiles,),
            in_specs=[inside] * (parts + 4) + [outside] * 2,
            out_specs=[inside] * outs,
            scratch_shapes=[
                pltpu.VMEM((tokens, width), BF16),
                pltpu.VMEM((tokens, width), BF16),
                pltpu.VMEM((tokens, width), F32),
                pltpu.VMEM((tokens, width), F32),
                pltpu.VMEM((tile, width), BF16),
                pltpu.VMEM((width, tile), BF16),
                pltpu.VMEM((depth, width, tile), BF16),
                pltpu.VMEM((depth, tile, width), BF16),
                pltpu.SemaphoreType.DMA((depth, 2)),
            ],
        ),
        out_shape=[out] * outs,
        compiler_params=pltpu.CompilerParams(
            dimension_semantics=("arbitrary",), vmem_limit_bytes=36 << 20
        ),
        cost_estimate=pl.CostEstimate(
            flops=8 * tokens * width * hidden,
            bytes_accessed=4 * width * hidden + 2 * tokens * hidden,
            transcendentals=0,
        ),
        name="section",
    )(me, *blocks, scale, saved, *first, w_in, w_out)


def sent(block, pipe_step, mp_xor):
    pipes, size = lax.axis_size("pipe"), lax.axis_size("mp")
    route = [
        (p * size + m, ((p + pipe_step) % pipes) * size + (m ^ mp_xor))
        for p in range(pipes)
        for m in range(size)
    ]
    return lax.ppermute(block, ("pipe", "mp"), route)


def onward(pair):
    return moved(pair, 0)


def moved(pair, mp_xor):
    if lax.axis_size("pipe") <= 2:
        return sent(pair, 1, mp_xor)
    return jnp.concatenate([sent(pair[:1], 1, mp_xor), sent(pair[1:], -1, mp_xor)])


def exchanged(own, size):
    blocks = {0: own}
    bit = size // 2
    while bit:
        for k in list(blocks):
            blocks[k ^ bit] = sent(blocks[k], 0, bit)
        bit //= 2
    return [blocks[k] for k in range(size)]


def rows_onward(three):
    if lax.axis_size("pipe") <= 2:
        return sent(three, 1, 0)
    return jnp.concatenate([sent(three[:1], 1, 0), sent(three[1:], -1, 0)])


def on_device(fwd_in, grad_in, saved_in, saved_hidden, gain, w_in, w_out):
    own, three, scale = packed(fwd_in[0], grad_in[0], saved_in[0], gain[0][None, :])
    shifted = rows_onward(three)
    size = lax.axis_size("mp")
    rows = own.shape[1]
    arrays = (saved_hidden[0], w_in[0], w_out[0])
    tile = tile_of(w_in.shape[2], 2048)
    first = first_tile(tile, *arrays[1:])
    if size & (size - 1) == 0 and size > 1 and rows % 16 == 0:
        me = jnp.full((1,), lax.axis_index("mp"), jnp.int32)
        keep, give = section(tile, me, exchanged(own, size), scale, first, *arrays)
        got = sent(give, 0, 1)
        total = jnp.zeros((2,) + own.shape[1:], F32)
        for k in range(size // 2):
            pair = (keep[k].astype(F32) + got[k].astype(F32)).astype(BF16)
            total = total + moved(pair, 2 * k).astype(F32)
    else:
        whole = lax.all_gather(own, "mp", axis=1, tiled=True)
        me = jnp.zeros((1,), jnp.int32)
        (part,) = section(tile, me, [whole], scale, first, *arrays)
        total = onward(lax.psum_scatter(part[0], "mp", scatter_dimension=1, tiled=True)).astype(F32)
    x, g, u = shifted
    section_out = (x.astype(F32) + total[0]).astype(BF16)
    uf = u.astype(F32)
    recip = lax.rsqrt(jnp.mean(uf * uf, axis=-1, keepdims=True) + EPS)
    scaled = total[1]
    inner = jnp.mean(scaled * uf, axis=-1, keepdims=True)
    input_grad = (g.astype(F32) + recip * scaled - uf * recip * recip * recip * inner).astype(BF16)
    return (section_out[None], input_grad[None])


def solution(mesh):
    rows = P("pipe", ("dp", "mp"), None)
    in_specs = (
        rows,
        rows,
        rows,
        P("pipe", "dp", "mp"),
        P("pipe", None),
        P("pipe", None, "mp"),
        P("pipe", "mp", None),
    )
    return jax.shard_map(
        on_device, mesh=mesh, in_specs=in_specs, out_specs=(rows, rows), check_vma=False
    )
```

```python
import functools

import jax
import jax.numpy as jnp
from jax import lax
from jax.experimental import pallas as pl
from jax.experimental.pallas import tpu as pltpu
from jax.sharding import PartitionSpec as P

EPS = 1e-06
F32 = jnp.float32
BF16 = jnp.bfloat16


def tile_of(extent, limit):
    size = limit
    while size > 128 and extent % size:
        size //= 2
    return size if extent % size == 0 else extent


def pack_kernel(x_ref, g_ref, u_ref, gain_ref, own_ref, all_ref, scale_ref):
    x, g = x_ref[...], g_ref[...]
    xf = x.astype(F32)
    r = lax.rsqrt(jnp.mean(xf * xf, axis=-1, keepdims=True) + EPS)
    own_ref[0] = (xf * r * gain_ref[...]).astype(BF16)
    own_ref[1] = g
    all_ref[0] = x
    all_ref[1] = g
    all_ref[2] = u_ref[...]
    scale_ref[...] = gain_ref[...]


def packed(x, g, u, gain):
    return pl.pallas_call(
        pack_kernel,
        out_shape=[
            pltpu.VMEM((2,) + x.shape, BF16),
            pltpu.VMEM((3,) + x.shape, BF16),
            pltpu.VMEM(gain.shape, F32),
        ],
        name="pack",
    )(x, g, u, gain)


def tile_copies(tile, at, sources, targets, sems):
    mask, wi, wo = sources
    cut = pl.ds(at * tile if isinstance(at, int) else pl.multiple_of(at * tile, tile), tile)
    return [
        pltpu.make_async_copy(mask.at[:, cut], targets[0], sems.at[0]),
        pltpu.make_async_copy(wi.at[:, cut], targets[1], sems.at[1]),
        pltpu.make_async_copy(wo.at[cut, :], targets[2], sems.at[2]),
    ]


def load_kernel(tile, *refs):
    copies = tile_copies(tile, 0, refs[:3], refs[3:6], refs[6])
    for copy in copies:
        copy.start()
    for copy in copies:
        copy.wait()


def first_tile(tile, saved, w_in, w_out):
    tokens, width = saved.shape[0], w_in.shape[0]
    shapes = [(tokens, tile), (width, tile), (tile, width)]
    return pl.pallas_call(
        functools.partial(load_kernel, tile),
        in_specs=[pl.BlockSpec(memory_space=pltpu.HBM)] * 3,
        out_specs=[pl.BlockSpec(memory_space=pltpu.VMEM)] * 3,
        out_shape=[pltpu.VMEM(shape, BF16) for shape in shapes],
        scratch_shapes=[pltpu.SemaphoreType.DMA((3,))],
        compiler_params=pltpu.CompilerParams(vmem_limit_bytes=24 << 20),
        cost_estimate=pl.CostEstimate(
            flops=0, bytes_accessed=sum(4 * a * b for a, b in shapes), transcendentals=0
        ),
        name="load",
    )(saved, w_in, w_out)


def section_kernel(tiles, tile, depth, rows, parts, outs, *refs):
    blocks, refs = refs[:parts], refs[parts:]
    scale_ref, refs = refs[0], refs[1:]
    first, sources, refs = refs[:3], refs[3:6], refs[6:]
    out_refs, refs = refs[:outs], refs[outs:]
    n_ref, g_ref, af, ab, wit, wot, s_buf, wi_buf, wo_buf, sems = refs
    step = pl.program_id(0)
    me = lax.axis_index("mp") if parts > 1 else 0

    def place(k):
        return pl.ds(pl.multiple_of((me ^ k) * rows, rows), rows)

    def fetch(at, slot):
        targets = (s_buf.at[slot], wi_buf.at[slot], wo_buf.at[slot])
        return tile_copies(tile, at, sources, targets, sems.at[slot])

    def compute(mask, wi, wo):
        half = tile // 2
        low, high = slice(0, half), slice(half, tile)

        def hidden(cut):
            h = jnp.dot(n_ref[...], wi[:, cut], preferred_element_type=F32)
            return jnp.maximum(h, 0.0).astype(BF16)

        def hidden_grad(cut):
            p = jnp.dot(g_ref[...], wot[:, cut], preferred_element_type=F32)
            return jnp.where(mask[:, cut] > 0, p, 0.0).astype(BF16)

        wot[:, low] = wo[low, :].T
        h = hidden(low)
        wit[low, :] = wi[:, low].T
        af[...] += jnp.dot(h, wo[low, :], preferred_element_type=F32)
        wot[:, high] = wo[high, :].T
        hg = hidden_grad(low)
        h = hidden(high)
        wit[high, :] = wi[:, high].T
        ab[...] += jnp.dot(hg, wit[low, :], preferred_element_type=F32)
        af[...] += jnp.dot(h, wo[high, :], preferred_element_type=F32)
        ab[...] += jnp.dot(hidden_grad(high), wit[high, :], preferred_element_type=F32)

    @pl.when(step == 0)
    def _():
        for at in range(1, min(depth + 1, tiles)):
            for copy in fetch(at, at % depth):
                copy.start()
        for k, block in enumerate(blocks):
            n_ref[place(k), :] = block[0]
            g_ref[place(k), :] = block[1]
        af[...] = jnp.zeros_like(af)
        ab[...] = jnp.zeros_like(ab)
        compute(*first)

    @pl.when(step > 0)
    def _():
        slot = lax.rem(step, depth)
        for copy in fetch(step, slot):
            copy.wait()
        compute(s_buf.at[slot], wi_buf.at[slot], wo_buf.at[slot])

        @pl.when(step + depth < tiles)
        def _():
            for copy in fetch(step + depth, slot):
                copy.start()

    @pl.when(step == tiles - 1)
    def _():
        for k in range(parts):
            out = out_refs[k % outs]
            out[k // outs, 0] = af[place(k), :].astype(BF16)
            out[k // outs, 1] = (ab[place(k), :] * scale_ref[...]).astype(BF16)


def section(tile, blocks, scale, first, saved, w_in, w_out):
    parts = len(blocks)
    _, rows, width = blocks[0].shape
    tokens = parts * rows
    hidden = w_in.shape[1]
    tiles = hidden // tile
    depth = 3
    outs = min(parts, 2)
    per = parts // outs
    inside = pl.BlockSpec(memory_space=pltpu.VMEM)
    outside = pl.BlockSpec(memory_space=pltpu.HBM)
    out = jax.ShapeDtypeStruct((per, 2, rows, width), BF16)
    return pl.pallas_call(
        functools.partial(section_kernel, tiles, tile, depth, rows, parts, outs),
        grid_spec=pltpu.PrefetchScalarGridSpec(
            num_scalar_prefetch=0,
            grid=(tiles,),
            in_specs=[inside] * (parts + 4) + [outside] * 3,
            out_specs=[inside] * outs,
            scratch_shapes=[
                pltpu.VMEM((tokens, width), BF16),
                pltpu.VMEM((tokens, width), BF16),
                pltpu.VMEM((tokens, width), F32),
                pltpu.VMEM((tokens, width), F32),
                pltpu.VMEM((tile, width), BF16),
                pltpu.VMEM((width, tile), BF16),
                pltpu.VMEM((depth, tokens, tile), BF16),
                pltpu.VMEM((depth, width, tile), BF16),
                pltpu.VMEM((depth, tile, width), BF16),
                pltpu.SemaphoreType.DMA((depth, 3)),
            ],
        ),
        out_shape=[out] * outs,
        compiler_params=pltpu.CompilerParams(
            dimension_semantics=("arbitrary",), vmem_limit_bytes=42 << 20
        ),
        cost_estimate=pl.CostEstimate(
            flops=8 * tokens * width * hidden,
            bytes_accessed=4 * width * hidden + 2 * tokens * hidden,
            transcendentals=0,
        ),
        name="section",
    )(*blocks, scale, *first, saved, w_in, w_out)


def sent(block, pipe_step, mp_xor):
    pipes, size = lax.axis_size("pipe"), lax.axis_size("mp")
    route = [
        (p * size + m, ((p + pipe_step) % pipes) * size + (m ^ mp_xor))
        for p in range(pipes)
        for m in range(size)
    ]
    return lax.ppermute(block, ("pipe", "mp"), route)


def onward(pair):
    return moved(pair, 0)


def moved(pair, mp_xor):
    if lax.axis_size("pipe") <= 2:
        return sent(pair, 1, mp_xor)
    return jnp.concatenate([sent(pair[:1], 1, mp_xor), sent(pair[1:], -1, mp_xor)])


def exchanged(own, size):
    blocks = {0: own}
    bit = size // 2
    while bit:
        for k in list(blocks):
            blocks[k ^ bit] = sent(blocks[k], 0, bit)
        bit //= 2
    return [blocks[k] for k in range(size)]


def rows_onward(three):
    if lax.axis_size("pipe") <= 2:
        return sent(three, 1, 0)
    return jnp.concatenate([sent(three[:1], 1, 0), sent(three[1:], -1, 0)])


def on_device(fwd_in, grad_in, saved_in, saved_hidden, gain, w_in, w_out):
    own, three, scale = packed(fwd_in[0], grad_in[0], saved_in[0], gain[0][None, :])
    shifted = rows_onward(three)
    size = lax.axis_size("mp")
    rows = own.shape[1]
    arrays = (saved_hidden[0], w_in[0], w_out[0])
    arrays = [pltpu.with_memory_space_constraint(array, pltpu.HBM) for array in arrays]
    tile = tile_of(w_in.shape[2], 2048)
    first = first_tile(tile, *arrays)
    first = [pltpu.with_memory_space_constraint(block, pltpu.VMEM) for block in first]
    if size & (size - 1) == 0 and size > 1 and rows % 16 == 0:
        keep, give = section(tile, exchanged(own, size), scale, first, *arrays)
        got = sent(give, 0, 1)
        total = jnp.zeros((2,) + own.shape[1:], F32)
        for k in range(size // 2):
            pair = (keep[k].astype(F32) + got[k].astype(F32)).astype(BF16)
            total = total + moved(pair, 2 * k).astype(F32)
    else:
        whole = lax.all_gather(own, "mp", axis=1, tiled=True)
        (part,) = section(tile, [whole], scale, first, *arrays)
        total = onward(lax.psum_scatter(part[0], "mp", scatter_dimension=1, tiled=True)).astype(F32)
    x, g, u = shifted
    section_out = (x.astype(F32) + total[0]).astype(BF16)
    uf = u.astype(F32)
    recip = lax.rsqrt(jnp.mean(uf * uf, axis=-1, keepdims=True) + EPS)
    scaled = total[1]
    inner = jnp.mean(scaled * uf, axis=-1, keepdims=True)
    input_grad = (g.astype(F32) + recip * scaled - uf * recip * recip * recip * inner).astype(BF16)
    return (section_out[None], input_grad[None])


def solution(mesh):
    rows = P("pipe", ("dp", "mp"), None)
    in_specs = (
        rows,
        rows,
        rows,
        P("pipe", "dp", "mp"),
        P("pipe", None),
        P("pipe", None, "mp"),
        P("pipe", "mp", None),
    )
    return jax.shard_map(
        on_device, mesh=mesh, in_specs=in_specs, out_specs=(rows, rows), check_vma=False
    )
```

```python
import functools

import jax
import jax.numpy as jnp
from jax import lax
from jax.experimental import pallas as pl
from jax.experimental.pallas import tpu as pltpu
from jax.sharding import PartitionSpec as P

EPS = 1e-06
F32 = jnp.float32
BF16 = jnp.bfloat16


def tile_of(extent, limit):
    size = limit
    while size > 128 and extent % size:
        size //= 2
    return size if extent % size == 0 else extent


def pack_kernel(x_ref, g_ref, u_ref, gain_ref, own_ref, all_ref, scale_ref):
    x, g = x_ref[...], g_ref[...]
    xf = x.astype(F32)
    r = lax.rsqrt(jnp.mean(xf * xf, axis=-1, keepdims=True) + EPS)
    own_ref[0] = (xf * r * gain_ref[...]).astype(BF16)
    own_ref[1] = g
    all_ref[0] = x
    all_ref[1] = g
    all_ref[2] = u_ref[...]
    scale_ref[...] = gain_ref[...]


def packed(x, g, u, gain):
    return pl.pallas_call(
        pack_kernel,
        out_shape=[
            pltpu.VMEM((2,) + x.shape, BF16),
            pltpu.VMEM((3,) + x.shape, BF16),
            pltpu.VMEM(gain.shape, F32),
        ],
        name="pack",
    )(x, g, u, gain)


def tile_copies(tile, at, sources, targets, sems):
    mask, wi, wo = sources
    cut = pl.ds(at * tile if isinstance(at, int) else pl.multiple_of(at * tile, tile), tile)
    return [
        pltpu.make_async_copy(mask.at[:, cut], targets[0], sems.at[0]),
        pltpu.make_async_copy(wi.at[:, cut], targets[1], sems.at[1]),
        pltpu.make_async_copy(wo.at[cut, :], targets[2], sems.at[2]),
    ]


def load_kernel(tile, *refs):
    copies = tile_copies(tile, 0, refs[:3], refs[3:6], refs[6])
    for copy in copies:
        copy.start()
    for copy in copies:
        copy.wait()


def first_tile(tile, saved, w_in, w_out):
    tokens, width = saved.shape[0], w_in.shape[0]
    shapes = [(tokens, tile), (width, tile), (tile, width)]
    return pl.pallas_call(
        functools.partial(load_kernel, tile),
        in_specs=[pl.BlockSpec(memory_space=pltpu.HBM)] * 3,
        out_specs=[pl.BlockSpec(memory_space=pltpu.VMEM)] * 3,
        out_shape=[pltpu.VMEM(shape, BF16) for shape in shapes],
        scratch_shapes=[pltpu.SemaphoreType.DMA((3,))],
        compiler_params=pltpu.CompilerParams(vmem_limit_bytes=24 << 20),
        cost_estimate=pl.CostEstimate(
            flops=0, bytes_accessed=sum(4 * a * b for a, b in shapes), transcendentals=0
        ),
        name="load",
    )(saved, w_in, w_out)


def section_kernel(tiles, tile, depth, rows, parts, outs, *refs):
    blocks, refs = refs[:parts], refs[parts:]
    scale_ref, refs = refs[0], refs[1:]
    first, sources, refs = refs[:3], refs[3:6], refs[6:]
    out_refs, refs = refs[:outs], refs[outs:]
    n_ref, g_ref, af, ab, wit, wot, s_buf, wi_buf, wo_buf, sems = refs
    step = pl.program_id(0)
    me = lax.axis_index("mp") if parts > 1 else 0

    def place(k):
        return pl.ds(pl.multiple_of((me ^ k) * rows, rows), rows)

    def fetch(at, slot):
        targets = (s_buf.at[slot], wi_buf.at[slot], wo_buf.at[slot])
        return tile_copies(tile, at, sources, targets, sems.at[slot])

    def compute(mask, wi, wo):
        half = tile // 2
        low, high = slice(0, half), slice(half, tile)

        def hidden(cut):
            h = jnp.dot(n_ref[...], wi[:, cut], preferred_element_type=F32)
            return jnp.maximum(h, 0.0).astype(BF16)

        def hidden_grad(cut):
            p = jnp.dot(g_ref[...], wot[:, cut], preferred_element_type=F32)
            return jnp.where(mask[:, cut] > 0, p, 0.0).astype(BF16)

        wot[:, low] = wo[low, :].T
        h = hidden(low)
        wit[low, :] = wi[:, low].T
        af[...] += jnp.dot(h, wo[low, :], preferred_element_type=F32)
        wot[:, high] = wo[high, :].T
        hg = hidden_grad(low)
        h = hidden(high)
        wit[high, :] = wi[:, high].T
        ab[...] += jnp.dot(hg, wit[low, :], preferred_element_type=F32)
        af[...] += jnp.dot(h, wo[high, :], preferred_element_type=F32)
        ab[...] += jnp.dot(hidden_grad(high), wit[high, :], preferred_element_type=F32)

    @pl.when(step == 0)
    def _():
        for at in range(1, min(depth + 1, tiles)):
            for copy in fetch(at, at % depth):
                copy.start()
        for k, block in enumerate(blocks):
            n_ref[place(k), :] = block[0]
            g_ref[place(k), :] = block[1]
        af[...] = jnp.zeros_like(af)
        ab[...] = jnp.zeros_like(ab)
        compute(*first)

    @pl.when(step > 0)
    def _():
        slot = lax.rem(step, depth)
        for copy in fetch(step, slot):
            copy.wait()
        compute(s_buf.at[slot], wi_buf.at[slot], wo_buf.at[slot])

        @pl.when(step + depth < tiles)
        def _():
            for copy in fetch(step + depth, slot):
                copy.start()

    @pl.when(step == tiles - 1)
    def _():
        for k in range(parts):
            out = out_refs[k % outs]
            out[k // outs, 0] = af[place(k), :].astype(BF16)
            out[k // outs, 1] = (ab[place(k), :] * scale_ref[...]).astype(BF16)


def section(tile, blocks, scale, first, saved, w_in, w_out):
    parts = len(blocks)
    _, rows, width = blocks[0].shape
    tokens = parts * rows
    hidden = w_in.shape[1]
    tiles = hidden // tile
    depth = 3
    outs = min(parts, 2)
    per = parts // outs
    inside = pl.BlockSpec(memory_space=pltpu.VMEM)
    outside = pl.BlockSpec(memory_space=pltpu.HBM)
    out = jax.ShapeDtypeStruct((per, 2, rows, width), BF16)
    return pl.pallas_call(
        functools.partial(section_kernel, tiles, tile, depth, rows, parts, outs),
        grid_spec=pltpu.PrefetchScalarGridSpec(
            num_scalar_prefetch=0,
            grid=(tiles,),
            in_specs=[inside] * (parts + 4) + [outside] * 3,
            out_specs=[inside] * outs,
            scratch_shapes=[
                pltpu.VMEM((tokens, width), BF16),
                pltpu.VMEM((tokens, width), BF16),
                pltpu.VMEM((tokens, width), F32),
                pltpu.VMEM((tokens, width), F32),
                pltpu.VMEM((tile, width), BF16),
                pltpu.VMEM((width, tile), BF16),
                pltpu.VMEM((depth, tokens, tile), BF16),
                pltpu.VMEM((depth, width, tile), BF16),
                pltpu.VMEM((depth, tile, width), BF16),
                pltpu.SemaphoreType.DMA((depth, 3)),
            ],
        ),
        out_shape=[out] * outs,
        compiler_params=pltpu.CompilerParams(
            dimension_semantics=("arbitrary",), vmem_limit_bytes=42 << 20
        ),
        cost_estimate=pl.CostEstimate(
            flops=8 * tokens * width * hidden,
            bytes_accessed=4 * width * hidden + 2 * tokens * hidden,
            transcendentals=0,
        ),
        name="section",
    )(*blocks, scale, *first, saved, w_in, w_out)


def sent(block, pipe_step, mp_xor):
    pipes, size = lax.axis_size("pipe"), lax.axis_size("mp")
    route = [
        (p * size + m, ((p + pipe_step) % pipes) * size + (m ^ mp_xor))
        for p in range(pipes)
        for m in range(size)
    ]
    return lax.ppermute(block, ("pipe", "mp"), route)


def onward(pair):
    return moved(pair, 0)


def moved(pair, mp_xor):
    if lax.axis_size("pipe") <= 2:
        return sent(pair, 1, mp_xor)
    return jnp.concatenate([sent(pair[:1], 1, mp_xor), sent(pair[1:], -1, mp_xor)])


def exchanged(own, size):
    blocks = {0: own}
    bit = size // 2
    while bit:
        for k in list(blocks):
            blocks[k ^ bit] = sent(blocks[k], 0, bit)
        bit //= 2
    return [blocks[k] for k in range(size)]


def rows_onward(three):
    if lax.axis_size("pipe") <= 2:
        return sent(three, 1, 0)
    return jnp.concatenate([sent(three[:1], 1, 0), sent(three[1:], -1, 0)])


def on_device(fwd_in, grad_in, saved_in, saved_hidden, gain, w_in, w_out):
    own, three, scale = packed(fwd_in[0], grad_in[0], saved_in[0], gain[0][None, :])
    shifted = rows_onward(three)
    size = lax.axis_size("mp")
    rows = own.shape[1]
    arrays = (saved_hidden[0], w_in[0], w_out[0])
    arrays = [pltpu.with_memory_space_constraint(array, pltpu.HBM) for array in arrays]
    tile = tile_of(w_in.shape[2], 2048)
    first = first_tile(tile, *arrays)
    first = [pltpu.with_memory_space_constraint(block, pltpu.VMEM) for block in first]
    if size & (size - 1) == 0 and size > 1 and rows % 16 == 0:
        keep, give = section(tile, exchanged(own, size), scale, first, *arrays)
        got = sent(give, 0, 1)

        def pair_sum(k, path):
            return (keep[k, path].astype(F32) + got[k, path].astype(F32)).astype(BF16)

        back = pair_sum(0, 1).astype(F32)
        ahead = jnp.zeros(own.shape[1:], F32)
        for k in range(1, size // 2):
            back = back + sent(pair_sum(k, 1), 0, 2 * k).astype(F32)
        for k in range(size // 2):
            ahead = ahead + sent(pair_sum(k, 0), 1, 2 * k).astype(F32)
        back = sent(back.astype(BF16), -1, 0).astype(F32)
        total = (ahead, back)
    else:
        whole = lax.all_gather(own, "mp", axis=1, tiled=True)
        (part,) = section(tile, [whole], scale, first, *arrays)
        total = onward(lax.psum_scatter(part[0], "mp", scatter_dimension=1, tiled=True)).astype(F32)
    x, g, u = shifted
    section_out = (x.astype(F32) + total[0]).astype(BF16)
    uf = u.astype(F32)
    recip = lax.rsqrt(jnp.mean(uf * uf, axis=-1, keepdims=True) + EPS)
    scaled = total[1]
    inner = jnp.mean(scaled * uf, axis=-1, keepdims=True)
    input_grad = (g.astype(F32) + recip * scaled - uf * recip * recip * recip * inner).astype(BF16)
    return (section_out[None], input_grad[None])


def solution(mesh):
    rows = P("pipe", ("dp", "mp"), None)
    in_specs = (
        rows,
        rows,
        rows,
        P("pipe", "dp", "mp"),
        P("pipe", None),
        P("pipe", None, "mp"),
        P("pipe", "mp", None),
    )
    return jax.shard_map(
        on_device, mesh=mesh, in_specs=in_specs, out_specs=(rows, rows), check_vma=False
    )
```
